1024 devices in a mesh: lon: 16 (over z), lat: 4 (over x_hi, core), mem: 16 (over x_lo, y).
Axes of the slice: x: 4 (x_hi: 2, x_lo: 2; x = x_hi * 2 + x_lo), y: 8, z: 16, core: 2. Of those that a mesh axis runs over, the one named last changes fastest.
Arguments:
- controls: float32 [64, 384, 96, 128], P('mem', 'lon', 'lat'), may hold values from -6 to 6
- ensemble: bfloat16 [64, 384, 96, 128], P('mem', 'lon', 'lat'), may hold values from -1.5 to 1.5
- taps_lon: float32 [17], replicated, may hold values from 0.05 to 0.35
- taps_lat: float32 [17], replicated, may hold values from 0.05 to 0.35
- obs_columns: int32 [16, 4, 16, 16], P('lon', 'lat', 'mem'), may hold values from 0 to 575
- obs_count: int32 [16, 4, 16], P('lon', 'lat', 'mem'), may hold values from 1 to 16, as said below
- obs_quality: int32 [16, 4, 16, 16], P('lon', 'lat', 'mem'), may hold values from 0 to 3
- obs_values: float32 [16, 4, 16, 16, 128], P('lon', 'lat', 'mem'), may hold values from -6 to 6
Outputs:
- new_controls: float32 [64, 384, 96, 128], P('mem', 'lon', 'lat')
- residual: float32 [16, 4, 16, 16, 128], P('lon', 'lat', 'mem')
The draws below stay inside these ranges and needn't reach their ends.
Inputs may be any that keep to these rules, and one draw needn't show every extreme that they name: `obs_columns`: column within the owner's tile, numbered as longitude offset times 24 plus latitude offset. `obs_count`: slots from this number on are unused; some owner has exactly 16 live slots.
All inputs are finite; a program needn't handle non-finite values.
Results may differ from the reference program's by a relative error of at most 0.0049.
Values may be sent and summed in bfloat16 or wider, within the bound.
A program may use at most 32 MiB of HBM per device.

```python
import jax
import jax.numpy as jnp
from jax import lax

LONX = 24
LATY = 24
LEV = 128
NOBS = 16
TAPS = 17
MEMBERS = 64
NLON = 384
NLAT = 96
TILES_LON = 16
TILES_LAT = 4
OWNERS = 16


def draw_obs_count(key, part):
    first, second = jax.random.split(key)
    choose = jax.random.randint(first, (TILES_LON, TILES_LAT, OWNERS), 0, 4)
    light = jax.random.randint(second, (TILES_LON, TILES_LAT, OWNERS), 1, NOBS // 4 + 1)
    counts = jnp.where(choose == 0, NOBS, light)
    return counts.at[0, 0, 0].set(NOBS).astype(jnp.int32)


def plant(values, own_key, least, high):
    place = [jax.random.randint(jax.random.fold_in(own_key, axis), (), 0, length) for axis, length in enumerate(values.shape)]
    widest = values.shape.index(max(values.shape))
    next_to = place[:widest] + [(place[widest] + 1) % values.shape[widest]] + place[widest + 1:]
    return values.at[tuple(place)].set(least).at[tuple(next_to)].set(high)


def level_of(key, shape, cuts, smallest, top_value):
    factor_of, own = 1.0, jax.random.fold_in(key, 6)
    for dim, blocks in cuts:
        draws = jnp.exp(jax.random.uniform(jax.random.fold_in(own, dim), (blocks,), jnp.float32, smallest / len(cuts), top_value / len(cuts)))
        factor_of = factor_of * jnp.repeat(draws, shape[dim] // blocks).reshape([-1 if axis == dim else 1 for axis in range(len(shape))])
    return factor_of


def scatter_about(own_key, shape, width, limit, shards=(), dtype=jnp.bfloat16):
    entries = jax.random.normal(own_key, shape, jnp.float32) * width
    if len(shards) > 0:
        entries = level_of(own_key, shape, shards, -0.22, 0.18) * entries
    return jnp.clip(entries, min=-limit, max=limit).astype(dtype)


def setup_inputs(seed: int = 0) -> dict:
    splits = jax.random.split(jax.random.key(seed), 9)
    return {
        "controls": scatter_about(splits[0], (MEMBERS, NLON, NLAT, LEV), 1.0, 6.0, ((0, 16), (1, 16), (2, 4)), jnp.float32),
        "ensemble": scatter_about(splits[1], (MEMBERS, NLON, NLAT, LEV), 0.25, 1.5, ((0, 16), (1, 16), (2, 4))),
        "taps_lon": jnp.clip(jax.random.uniform(splits[2], (TAPS,), jnp.float32, 0.05, 0.35), 0.05, 0.35),
        "taps_lat": jnp.clip(jax.random.uniform(splits[3], (TAPS,), jnp.float32, 0.05, 0.35), 0.05, 0.35),
        "obs_columns": plant(jax.random.randint(splits[4], (TILES_LON, TILES_LAT, OWNERS, NOBS), 0, LONX * LATY), jax.random.fold_in(splits[4], 1), 0, (LONX * LATY) - 1).astype(jnp.int32),
        "obs_count": draw_obs_count(jax.random.fold_in(splits[8], 71), 0),
        "obs_quality": plant(jax.random.randint(splits[6], (TILES_LON, TILES_LAT, OWNERS, NOBS), 0, 4), jax.random.fold_in(splits[6], 1), 0, 3).astype(jnp.int32),
        "obs_values": scatter_about(splits[7], (TILES_LON, TILES_LAT, OWNERS, NOBS, LEV), 1.0, 6.0, ((0, 16), (1, 4), (2, 16)), jnp.float32),
    }


descent = 0.5


def rounded(value):
    return lax.optimization_barrier(value.astype(jnp.bfloat16)).astype(jnp.float32)


def lon_conv(field, kernel):
    tap_count = kernel.shape[0]
    rim_width = tap_count // 2
    result = jnp.zeros_like(field)
    for tap_index in range(tap_count):
        result = result + kernel[tap_index] * jnp.roll(field, rim_width - tap_index, axis=0)
    return result


def lat_conv(field, kernel):
    tap_count = kernel.shape[0]
    rim_width = tap_count // 2
    width_lat = field.shape[1]
    padded = jnp.pad(field, ((0, 0), (rim_width, rim_width), (0, 0)))
    result = jnp.zeros_like(field)
    for tap_index in range(tap_count):
        result = result + kernel[tap_index] * padded[:, tap_index:tap_index + width_lat]
    return result


def pick_rows(tile_grid, picked):
    return tile_grid[picked]


def spread_back(values, picked):
    return jnp.zeros((LONX * LATY, LEV), jnp.float32).at[picked].add(values)


def reference(controls, ensemble, taps_lon, taps_lat, obs_columns, obs_count, obs_quality, obs_values):
    kernel_lon = rounded(taps_lon)
    kernel_lat = rounded(taps_lat)

    def accumulate(total, pair):
        control, member = pair
        spread = lat_conv(rounded(lon_conv(rounded(control), kernel_lon)), kernel_lat)
        return total + member.astype(jnp.float32) * spread, None

    increment, _ = lax.scan(accumulate, jnp.zeros((NLON, NLAT, LEV), jnp.float32), (controls, ensemble))
    tiled = increment.reshape(TILES_LON, LONX, TILES_LAT, LATY, LEV).transpose(0, 2, 1, 3, 4)
    tiled = tiled.reshape(TILES_LON * TILES_LAT, LONX * LATY, LEV)
    columns = obs_columns.reshape(TILES_LON * TILES_LAT, OWNERS * NOBS)
    observed = jax.vmap(pick_rows)(tiled, columns).reshape(TILES_LON, TILES_LAT, OWNERS, NOBS, LEV)
    active = jnp.arange(NOBS)[None, None, None, :] < obs_count[..., None]
    weights = jnp.where(active, 0.5 * obs_quality.astype(jnp.float32), jnp.zeros((), jnp.float32))
    residual = weights[..., None] * (observed - obs_values)
    adjoint_tiles = jax.vmap(spread_back)(residual.reshape(TILES_LON * TILES_LAT, OWNERS * NOBS, LEV), columns)
    adjoint = adjoint_tiles.reshape(TILES_LON, TILES_LAT, LONX, LATY, LEV).transpose(0, 2, 1, 3, 4)
    adjoint = adjoint.reshape(NLON, NLAT, LEV)
    flip_lon = kernel_lon[::-1]
    flip_lat = kernel_lat[::-1]

    def update(pair):
        control, member = pair
        product = rounded(member.astype(jnp.float32) * adjoint)
        lon_back = lon_conv(rounded(lat_conv(product, flip_lat)), flip_lon)
        return control - descent * (control + lon_back)

    new_controls = lax.map(update, (controls, ensemble))
    return new_controls, residual
```

```python
import functools

import jax
import jax.numpy as jnp
from jax import lax
from jax.experimental import pallas as pl
from jax.experimental.pallas import tpu as pltpu
from jax.sharding import PartitionSpec as P

LEV = 128
TILE = 24
HALF = 8
TAPS = 17
SLOTS = 16
MEM = 4
WIDE = MEM * LEV
CELLS = TILE * TILE
SIDE = TILE * HALF
CORNER = HALF * HALF
descent = 0.5
OFF_Z = 0
OFF_L = 2 * SIDE
OFF_X = 4 * SIDE
OFF_C = 4 * SIDE + 4 * CORNER
EXT = OFF_C + CELLS + 64
PAD_C = CELLS + 64
REGIONS = (
    (-1, 0, OFF_Z, SIDE),
    (1, 0, OFF_Z + SIDE, SIDE),
    (0, -1, OFF_L, SIDE),
    (0, 1, OFF_L + SIDE, SIDE),
    (-1, -1, OFF_X, CORNER),
    (1, -1, OFF_X + CORNER, CORNER),
    (-1, 1, OFF_X + 2 * CORNER, CORNER),
    (1, 1, OFF_X + 3 * CORNER, CORNER),
)
GROUPS = ((0, 2, OFF_Z, 2 * SIDE), (2, 4, OFF_L, 2 * SIDE), (4, 8, OFF_X, 4 * CORNER))
MESH = pl.DeviceIdType.MESH
f32 = jnp.float32
bf16 = jnp.bfloat16


def iota(shape, dim):
    return lax.broadcasted_iota(jnp.int32, shape, dim)


def by_tile(q):
    i = (q * 2731) >> 16
    return i, q - TILE * i


def column_coords():
    lon, lat = [], []
    def add(i, j):
        lon.append(i)
        lat.append(j)
    for base in (0, HALF + TILE):
        i, j = by_tile(iota((1, SIDE), 1))
        add(i + base, j + HALF)
    for base in (0, HALF + TILE):
        q = iota((1, SIDE), 1)
        add((q >> 3) + HALF, (q & 7) + base)
    for base_lat in (0, HALF + TILE):
        for base_lon in (0, HALF + TILE):
            q = iota((1, CORNER), 1)
            add((q >> 3) + base_lon, (q & 7) + base_lat)
    i, j = by_tile(iota((1, PAD_C), 1))
    ok = iota((1, PAD_C), 1) < CELLS
    add(jnp.where(ok, i + HALF, -1), jnp.where(ok, j + HALF, -1))
    return jnp.concatenate(lon, axis=1), jnp.concatenate(lat, axis=1)


def dot(a, b):
    return jnp.dot(a, b, preferred_element_type=f32)


def piece(dz, dl, field):
    i0, ni = {-1: (TILE - HALF, HALF), 1: (0, HALF), 0: (0, TILE)}[dz]
    j0 = {-1: TILE - HALF, 1: 0}[dl]
    part = field[i0:i0 + ni, j0:j0 + HALF, :]
    return part.reshape(ni * HALF, part.shape[2])


def kernel(sizes, ctrl_hbm, ens_hbm, tlon, tlat, cols, count, qual, vals, lb_ref, res_ref,
           ctrl, xall, eall, aall, xstage, estage, azs, astage, colall, gsend, grecv, rall, w2, k2, st, tabs, ensobs, acc,
           load_sem, rim_send, rim_recv, mem_send, mem_recv):
    n_lon, n_lat, n_mem = sizes
    z = lax.axis_index("lon")
    l = lax.axis_index("lat")
    me = lax.axis_index("mem")

    loads = [pltpu.make_async_copy(ctrl_hbm.at[m], ctrl.at[:, m * LEV:(m + 1) * LEV], load_sem.at[m]) for m in range(MEM)]
    loads_e = [
        pltpu.make_async_copy(ens_hbm.at[m], eall.at[OFF_C:OFF_C + CELLS, m * LEV:(m + 1) * LEV], load_sem.at[MEM + m])
        for m in range(MEM)
    ]
    for c in loads + loads_e:
        c.start()

    def lon_of(dz):
        return lax.rem(z + dz + n_lon, n_lon)

    def has(dl):
        if dl == 0:
            return None
        return (l + dl >= 0) & (l + dl < n_lat)

    def guarded(cond, f):
        if cond is None:
            f()
        else:
            pl.when(cond)(f)

    barrier = pltpu.get_barrier_semaphore()
    for dz, dl, _, _ in REGIONS:
        def greet(dz=dz, dl=dl):
            pl.semaphore_signal(barrier, inc=1, device_id={"lon": lon_of(dz), "lat": l + dl}, device_id_type=MESH)
        guarded(has(dl), greet)

    def greet_mem(t, _):
        pl.semaphore_signal(barrier, inc=1, device_id={"mem": lax.rem(me + t, n_mem)}, device_id_type=MESH)
        return 0
    lax.fori_loop(1, n_mem, greet_mem, 0)

    slot = iota((SLOTS, LEV), 0)
    col = jnp.zeros((SLOTS, LEV), jnp.int32)
    quality = jnp.zeros((SLOTS, LEV), f32)
    for s in range(SLOTS):
        col = jnp.where(slot == s, cols[s], col)
        quality = jnp.where(slot == s, qual[s].astype(f32), quality)
    weights = jnp.where(slot < count[0], 0.5 * quality, 0.0)
    mine = pl.ds(pl.multiple_of(me * SLOTS, SLOTS), SLOTS)
    colall[mine, :] = col

    for c in loads:
        c.wait()
    field = ctrl[...]
    xall[OFF_C:OFF_C + CELLS, :] = field.astype(bf16)
    xall[OFF_C + CELLS:EXT, :] = jnp.zeros((64, WIDE), bf16)
    eall[OFF_C + CELLS:EXT, :] = jnp.zeros((64, WIDE), bf16)
    field = field.reshape(TILE, TILE, WIDE)
    for dz, dl, row, rows in REGIONS[2:]:
        xstage[row - OFF_L:row - OFF_L + rows, :] = piece(dz, dl, field).astype(bf16)

    for dl, row, xrow in ((-1, OFF_L, OFF_X), (1, OFF_L + SIDE, OFF_X + 2 * CORNER)):
        @pl.when(jnp.logical_not(has(dl)))
        def _(row=row, xrow=xrow):
            for ref in (xall, eall):
                ref[row:row + SIDE, :] = jnp.zeros((SIDE, WIDE), bf16)
                ref[xrow:xrow + 2 * CORNER, :] = jnp.zeros((2 * CORNER, WIDE), bf16)
            aall[row:row + SIDE, :] = jnp.zeros((SIDE, LEV), bf16)
            aall[xrow:xrow + 2 * CORNER, :] = jnp.zeros((2 * CORNER, LEV), bf16)

    both = jnp.where((l > 0) & (l < n_lat - 1), 8, 5)
    pl.semaphore_wait(barrier, both + n_mem - 1)

    def rim_copy(kind, d, own, own_row, stage, dst):
        dz, dl, row, rows = REGIONS[d]
        if dl == 0:
            first = own_row + (CELLS - SIDE if dz == -1 else 0)
            src = own.at[first:first + rows, :]
        else:
            src = stage.at[row - OFF_L:row - OFF_L + rows, :]
        return pltpu.make_async_remote_copy(
            src_ref=src, dst_ref=dst.at[row:row + rows, :],
            send_sem=rim_send.at[kind, d], recv_sem=rim_recv.at[kind, d],
            device_id={"lon": lon_of(-dz), "lat": l - dl}, device_id_type=MESH)

    def start_rims(copies):
        for d, c in enumerate(copies):
            guarded(has(-REGIONS[d][1]), c.start)

    def recv_rims(copies, lo, hi):
        for d in range(lo, hi):
            guarded(has(REGIONS[d][1]), copies[d].wait_recv)

    def sent_rims(copies):
        for d, c in enumerate(copies):
            guarded(has(-REGIONS[d][1]), c.wait_send)

    def rows_of(index):
        return pl.ds(pl.multiple_of(index * SLOTS, SLOTS), SLOTS)

    def mem_copy(kind, t, src_of, dst):
        peer = lax.rem(me + t, n_mem)
        return pltpu.make_async_remote_copy(
            src_ref=src_of(peer), dst_ref=dst.at[mine, :],
            send_sem=mem_send.at[kind, t], recv_sem=mem_recv.at[kind, t],
            device_id={"mem": peer}, device_id_type=MESH)

    def mem_loop(kind, src_of, dst, what):
        def step(t, _):
            getattr(mem_copy(kind, t, src_of, dst), what)()
            return 0
        lax.fori_loop(1, n_mem, step, 0)

    col_of = lambda peer: colall.at[mine, :]
    g_of = lambda peer: gsend.at[rows_of(peer), :]
    r_of = lambda peer: rall.at[mine, :]

    xrims = [rim_copy(0, d, xall, OFF_C, xstage, xall) for d in range(8)]
    erims = [rim_copy(1, d, eall, OFF_C, estage, eall) for d in range(8)]
    arims = [rim_copy(2, d, azs, 0, astage, aall) for d in range(8)]

    mem_loop(0, col_of, colall, "start")
    start_rims(xrims)

    for c in loads_e:
        c.wait()
    field = eall[OFF_C:OFF_C + CELLS, :].astype(f32).reshape(TILE, TILE, WIDE)
    for dz, dl, row, rows in REGIONS[2:]:
        estage[row - OFF_L:row - OFF_L + rows, :] = piece(dz, dl, field).astype(bf16)
    start_rims(erims)

    shift = iota((32, 48), 1) - iota((32, 48), 0)
    lon_q, lat_q = column_coords()
    for index, (tap, coord) in enumerate(((tlon, lon_q), (tlat, lat_q))):
        here = jnp.where(iota((48, EXT), 0) == jnp.broadcast_to(coord, (48, EXT)), 1.0, 0.0).astype(bf16)
        ahead = jnp.zeros((32, 48), f32)
        back = jnp.zeros((32, 48), f32)
        for k in range(TAPS):
            ahead = jnp.where(shift == k, tap[k], ahead)
            back = jnp.where(shift == k, tap[TAPS - 1 - k], back)
        if index == 1:
            back = -descent * back
        tabs[index] = dot(ahead.astype(bf16), here).astype(bf16)
        tabs[2 + index] = dot(back.astype(bf16), here).astype(bf16)

    mem_loop(0, col_of, colall, "wait_recv")
    total = n_mem * SLOTS
    column = colall[...]
    own_i, own_j = by_tile(column)
    lane = iota((total, LEV), 1)
    pick_i = jnp.where(lane == own_i, 1.0, 0.0).astype(bf16)[:, :32]
    pick_j = jnp.where(lane == own_j, 1.0, 0.0).astype(bf16)[:, :32]
    for q in range(0, EXT, 128):
        part = dot(pick_i, tabs[0, :, q:q + 128]) * dot(pick_j, tabs[1, :, q:q + 128])
        w2[:, q:q + 128] = part.astype(bf16)
    select = jnp.concatenate(
        [jnp.where(lane + q == column, 1.0, 0.0).astype(bf16) for q in range(0, PAD_C, 128)], axis=1)
    ensobs[...] = dot(select, eall[OFF_C:EXT, :])
    column_t = jnp.transpose(column.astype(f32))[0:1, :]
    cell = iota((CELLS, total), 0).astype(f32)
    st[...] = jnp.where(cell == jnp.broadcast_to(column_t, (CELLS, total)), 1.0, 0.0).astype(bf16)

    acc[...] = dot(w2[:, OFF_C:EXT], xall[OFF_C:EXT, :])
    for lo, hi, row, rows in GROUPS:
        recv_rims(xrims, lo, hi)
        acc[...] += dot(w2[:, row:row + rows], xall[row:row + rows, :])
    product = acc[...] * ensobs[...]
    part = product[:, 0:LEV]
    for m in range(1, MEM):
        part = part + product[:, m * LEV:(m + 1) * LEV]
    gsend[...] = part.astype(bf16)
    mem_loop(1, g_of, grecv, "start")
    grecv[mine, :] = gsend[mine, :]

    def build(b, _):
        rows = pl.ds(pl.multiple_of(b * 64, 64), 64)
        r = iota((64, 32), 0) + b * 64
        i, j = by_tile(r)
        lanes = iota((64, 32), 1)
        at_i = jnp.where(lanes == i, 1.0, 0.0).astype(bf16)
        at_j = jnp.where(lanes == j, 1.0, 0.0).astype(bf16)
        for q in range(0, EXT, 128):
            part = dot(at_i, tabs[2, :, q:q + 128]) * dot(at_j, tabs[3, :, q:q + 128])
            k2[rows, q:q + 128] = part.astype(bf16)
        return 0
    lax.fori_loop(0, CELLS // 64, build, 0)

    mem_loop(1, g_of, grecv, "wait_recv")
    observed = jnp.zeros((SLOTS, LEV), f32)
    for o in range(n_mem):
        observed = observed + grecv[o * SLOTS:(o + 1) * SLOTS, :].astype(f32)
    residual = weights * (observed - vals[...])
    res_ref[...] = residual
    rall[mine, :] = residual.astype(bf16)
    mem_loop(2, r_of, rall, "start")
    recv_rims(erims, 0, 8)
    mem_loop(2, r_of, rall, "wait_recv")

    adjoint = dot(st[...], rall[...])
    azs[...] = adjoint.astype(bf16)
    field = adjoint.reshape(TILE, TILE, LEV)
    for dz, dl, row, rows in REGIONS[2:]:
        astage[row - OFF_L:row - OFF_L + rows, :] = piece(dz, dl, field).astype(bf16)
    start_rims(arims)

    def backward(row, rows, adj):
        wide = jnp.concatenate([adj] * MEM, axis=1)
        weighted = (eall[row:row + rows, :].astype(f32) * wide).astype(bf16)
        return dot(k2[:, row:row + rows], weighted)

    zero = jnp.zeros((PAD_C - CELLS, LEV), f32)
    back = backward(OFF_C, PAD_C, jnp.concatenate([adjoint, zero], axis=0))
    for m in range(MEM):
        lb_ref[m] = back[:, m * LEV:(m + 1) * LEV].reshape(TILE, TILE, LEV)
    for lo, hi, row, rows in GROUPS:
        recv_rims(arims, lo, hi)
        back = backward(row, rows, aall[row:row + rows, :].astype(f32))
        for m in range(MEM):
            lb_ref[m] += back[:, m * LEV:(m + 1) * LEV].reshape(TILE, TILE, LEV)

    for copies in (xrims, erims, arims):
        sent_rims(copies)
    mem_loop(0, col_of, colall, "wait_send")
    mem_loop(1, g_of, grecv, "wait_send")
    mem_loop(2, r_of, rall, "wait_send")


def shards(sizes, controls, ensemble, taps_lon, taps_lat, obs_columns, obs_count, obs_quality, obs_values):
    total = sizes[2] * SLOTS
    smem = pl.BlockSpec(memory_space=pltpu.SMEM)
    vmem = pl.BlockSpec(memory_space=pltpu.VMEM)
    hbm = pl.BlockSpec(memory_space=pl.ANY)
    step, residual = pl.pallas_call(
        functools.partial(kernel, sizes),
        out_shape=(jax.ShapeDtypeStruct((MEM, TILE, TILE, LEV), f32), jax.ShapeDtypeStruct((SLOTS, LEV), f32)),
        in_specs=[hbm, hbm, smem, smem, smem, smem, smem, vmem],
        out_specs=(vmem, vmem),
        scratch_shapes=[
            pltpu.VMEM((CELLS, WIDE), f32),
            pltpu.VMEM((EXT, WIDE), bf16),
            pltpu.VMEM((EXT, WIDE), bf16),
            pltpu.VMEM((EXT, LEV), bf16),
            pltpu.VMEM((OFF_C - OFF_L, WIDE), bf16),
            pltpu.VMEM((OFF_C - OFF_L, WIDE), bf16),
            pltpu.VMEM((CELLS, LEV), bf16),
            pltpu.VMEM((OFF_C - OFF_L, LEV), bf16),
            pltpu.VMEM((total, LEV), jnp.int32),
            pltpu.VMEM((total, LEV), bf16),
            pltpu.VMEM((total, LEV), bf16),
            pltpu.VMEM((total, LEV), bf16),
            pltpu.VMEM((total, EXT), bf16),
            pltpu.VMEM((CELLS, EXT), bf16),
            pltpu.VMEM((CELLS, total), bf16),
            pltpu.VMEM((4, 32, EXT), bf16),
            pltpu.VMEM((total, WIDE), f32),
            pltpu.VMEM((total, WIDE), f32),
            pltpu.SemaphoreType.DMA((2 * MEM,)),
            pltpu.SemaphoreType.DMA((3, 8)),
            pltpu.SemaphoreType.DMA((3, 8)),
            pltpu.SemaphoreType.DMA((3, sizes[2])),
            pltpu.SemaphoreType.DMA((3, sizes[2])),
        ],
        compiler_params=pltpu.CompilerParams(collective_id=0, has_side_effects=True, vmem_limit_bytes=63 * 1024 * 1024),
        name="step",
    )(
        controls.reshape(MEM, CELLS, LEV),
        ensemble.reshape(MEM, CELLS, LEV),
        taps_lon,
        taps_lat,
        obs_columns.reshape(SLOTS),
        obs_count.reshape(1),
        obs_quality.reshape(SLOTS),
        obs_values.reshape(SLOTS, LEV),
    )
    new_controls = (1.0 - descent) * controls + step
    return new_controls, residual.reshape(obs_values.shape)


def solution(mesh):
    sizes = (mesh.shape["lon"], mesh.shape["lat"], mesh.shape["mem"])
    placed = (
        P("mem", "lon", "lat", None),
        P("mem", "lon", "lat", None),
        P(),
        P(),
        P("lon", "lat", "mem", None),
        P("lon", "lat", "mem"),
        P("lon", "lat", "mem", None),
        P("lon", "lat", "mem", None, None),
    )
    return jax.shard_map(
        functools.partial(shards, sizes),
        mesh=mesh,
        in_specs=placed,
        out_specs=(P("mem", "lon", "lat", None), P("lon", "lat", "mem", None, None)),
        check_vma=False,
    )
```

```python
import functools

import jax
import jax.numpy as jnp
from jax import lax
from jax.experimental import pallas as pl
from jax.experimental.pallas import tpu as pltpu
from jax.sharding import PartitionSpec as P

LEV = 128
TILE = 24
HALF = 8
TAPS = 17
SLOTS = 16
MEM = 4
WIDE = MEM * LEV
CELLS = TILE * TILE
SIDE = TILE * HALF
CORNER = HALF * HALF
descent = 0.5
OFF_Z = 0
OFF_L = 2 * SIDE
OFF_X = 4 * SIDE
OFF_C = 4 * SIDE + 4 * CORNER
EXT = OFF_C + CELLS + 64
PAD_C = CELLS + 64
REGIONS = (
    (-1, 0, OFF_Z, SIDE),
    (1, 0, OFF_Z + SIDE, SIDE),
    (0, -1, OFF_L, SIDE),
    (0, 1, OFF_L + SIDE, SIDE),
    (-1, -1, OFF_X, CORNER),
    (1, -1, OFF_X + CORNER, CORNER),
    (-1, 1, OFF_X + 2 * CORNER, CORNER),
    (1, 1, OFF_X + 3 * CORNER, CORNER),
)
GROUPS = ((0, 2, OFF_Z, 2 * SIDE), (2, 4, OFF_L, 2 * SIDE), (4, 8, OFF_X, 4 * CORNER))
MESH = pl.DeviceIdType.MESH
f32 = jnp.float32
bf16 = jnp.bfloat16


def iota(shape, dim):
    return lax.broadcasted_iota(jnp.int32, shape, dim)


def by_tile(q):
    i = (q * 2731) >> 16
    return i, q - TILE * i


def column_coords():
    lon, lat = [], []
    def add(i, j):
        lon.append(i)
        lat.append(j)
    for base in (0, HALF + TILE):
        i, j = by_tile(iota((1, SIDE), 1))
        add(i + base, j + HALF)
    for base in (0, HALF + TILE):
        q = iota((1, SIDE), 1)
        add((q >> 3) + HALF, (q & 7) + base)
    for base_lat in (0, HALF + TILE):
        for base_lon in (0, HALF + TILE):
            q = iota((1, CORNER), 1)
            add((q >> 3) + base_lon, (q & 7) + base_lat)
    i, j = by_tile(iota((1, PAD_C), 1))
    ok = iota((1, PAD_C), 1) < CELLS
    add(jnp.where(ok, i + HALF, -1), jnp.where(ok, j + HALF, -1))
    return jnp.concatenate(lon, axis=1), jnp.concatenate(lat, axis=1)


def dot(a, b):
    return jnp.dot(a, b, preferred_element_type=f32)


def piece(dz, dl, field):
    i0, ni = {-1: (TILE - HALF, HALF), 1: (0, HALF), 0: (0, TILE)}[dz]
    j0 = {-1: TILE - HALF, 1: 0}[dl]
    part = field[i0:i0 + ni, j0:j0 + HALF, :]
    return part.reshape(ni * HALF, part.shape[2])


def region_coords(d, n):
    dz, dl, _, _ = REGIONS[d]
    start = {-1: 0, 0: HALF, 1: HALF + TILE}
    q = iota((1, n), 1)
    i, j = by_tile(q) if dl == 0 else (q >> 3, q & 7)
    return i + start[dz], j + start[dl]


def block_of(ref, m, d):
    dz, dl, _, _ = REGIONS[d]
    part = {-1: slice(0, HALF), 0: slice(0, TILE), 1: slice(TILE - HALF, TILE)}
    return ref.at[m, part[dz], part[dl], :]


def one_hot(index, n):
    return jnp.where(iota((index.shape[0], n), 1) == index, 1.0, 0.0).astype(bf16)


def kernel(sizes, ctrl_hbm, ens_hbm, tlon_hbm, tlat_hbm, cols_hbm, count, qual_hbm, vals_hbm, out_ref, res_ref,
           ctrl, xall, eall, aall, xstage, estage, azs, astage, colall, gsend, grecv, rall, w2, k2c, k2z, k2l, k2x, st, tabs,
           back_tabs, ensobs, acc, tlon, tlat, cols, qual, vals,
           load_sem, small_sem, rim_send, rim_recv, mem_send, mem_recv):
    n_lon, n_lat, n_mem = sizes
    n_y = n_mem // 2
    z = lax.axis_index("lon")
    l = lax.axis_index("lat")
    me = lax.axis_index("mem")
    my_x, my_y = me // n_y, lax.rem(me, n_y)

    def lon_of(dz):
        return lax.rem(z + dz + n_lon, n_lon)

    def has(dl):
        if dl == 0:
            return None
        return (l + dl >= 0) & (l + dl < n_lat)

    def guarded(cond, f):
        if cond is None:
            f()
        else:
            pl.when(cond)(f)

    steps = [(dx, dy) for dy in sorted(range(n_y), key=lambda y: -min(y, n_y - y)) for dx in (1, 0)]
    steps = [s for s in steps if s != (0, 0)]

    def peer_of(dx, dy):
        return lax.rem(my_x + dx, 2) * n_y + lax.rem(my_y + dy, n_y)

    barrier = pltpu.get_barrier_semaphore()
    for dx, dy in steps:
        pl.semaphore_signal(barrier, inc=1, device_id={"mem": peer_of(dx, dy)}, device_id_type=MESH)
    for dz, dl, _, _ in REGIONS:
        def greet(dz=dz, dl=dl):
            pl.semaphore_signal(barrier, inc=1, device_id={"lon": lon_of(dz), "lat": l + dl}, device_id_type=MESH)
        guarded(has(dl), greet)

    loads = [pltpu.make_async_copy(ctrl_hbm.at[m], ctrl.at[:, m * LEV:(m + 1) * LEV], load_sem.at[m]) for m in range(MEM)]
    loads_e = [
        pltpu.make_async_copy(ens_hbm.at[m], eall.at[OFF_C:OFF_C + CELLS, m * LEV:(m + 1) * LEV], load_sem.at[MEM + m])
        for m in range(MEM)
    ]
    pairs = ((cols_hbm, cols), (qual_hbm, qual), (tlon_hbm, tlon), (tlat_hbm, tlat), (vals_hbm, vals))
    small = [pltpu.make_async_copy(a, b, small_sem.at[k]) for k, (a, b) in enumerate(pairs)]
    for c in loads + small + loads_e:
        c.start()

    xall[OFF_C + CELLS:EXT, :] = jnp.zeros((64, WIDE), bf16)
    eall[OFF_C + CELLS:EXT, :] = jnp.zeros((64, WIDE), bf16)
    for dl, row, xrow in ((-1, OFF_L, OFF_X), (1, OFF_L + SIDE, OFF_X + 2 * CORNER)):
        @pl.when(jnp.logical_not(has(dl)))
        def _(row=row, xrow=xrow):
            for ref in (xall, eall):
                ref[row:row + SIDE, :] = jnp.zeros((SIDE, WIDE), bf16)
                ref[xrow:xrow + 2 * CORNER, :] = jnp.zeros((2 * CORNER, WIDE), bf16)
            aall[row:row + SIDE, :] = jnp.zeros((SIDE, LEV), bf16)
            aall[xrow:xrow + 2 * CORNER, :] = jnp.zeros((2 * CORNER, LEV), bf16)

    for c in small:
        c.wait()
    lane1 = iota((1, LEV), 1)
    col = jnp.zeros((1, LEV), jnp.int32)
    for s in range(SLOTS):
        col = jnp.where(lane1 == s, cols[0, 0, 0, s], col)
    colall[me] = col

    for c in loads:
        c.wait()
    field = ctrl[...]
    xall[OFF_C:OFF_C + CELLS, :] = field.astype(bf16)
    field = field.reshape(TILE, TILE, WIDE)
    for dz, dl, row, rows in REGIONS[2:]:
        xstage[row - OFF_L:row - OFF_L + rows, :] = piece(dz, dl, field).astype(bf16)

    both = jnp.where((l > 0) & (l < n_lat - 1), 8, 5)
    pl.semaphore_wait(barrier, both + n_mem - 1)

    def rim_copy(kind, d, own, own_row, stage, dst):
        dz, dl, row, rows = REGIONS[d]
        if dl == 0:
            first = own_row + (CELLS - SIDE if dz == -1 else 0)
            src = own.at[first:first + rows, :]
        else:
            src = stage.at[row - OFF_L:row - OFF_L + rows, :]
        return pltpu.make_async_remote_copy(
            src_ref=src, dst_ref=dst.at[row:row + rows, :],
            send_sem=rim_send.at[kind, d], recv_sem=rim_recv.at[kind, d],
            device_id={"lon": lon_of(-dz), "lat": l - dl}, device_id_type=MESH)

    def crosses(d):
        return lax.rem(l, 2) == (1 if REGIONS[d][1] == -1 else 0)

    def start_rims(copies):
        for d, c in enumerate(copies):
            guarded(has(-REGIONS[d][1]), c.start)

    def start_some(copies, which, across):
        for d in which:
            dl = REGIONS[d][1]
            if dl == 0:
                if not across:
                    copies[d].start()
            else:
                far = crosses(d)
                guarded(has(-dl) & (far if across else jnp.logical_not(far)), copies[d].start)

    def recv_rims(copies, lo, hi):
        for d in range(lo, hi):
            guarded(has(REGIONS[d][1]), copies[d].wait_recv)

    def sent_rims(copies):
        for d, c in enumerate(copies):
            guarded(has(-REGIONS[d][1]), c.wait_send)

    def rows_of(index):
        return pl.ds(pl.multiple_of(index * SLOTS, SLOTS), SLOTS)

    mine = rows_of(me)

    def mem_copies(kind, src_of, dst):
        made = []
        for t, (dx, dy) in enumerate(steps):
            peer = peer_of(dx, dy)
            made.append(pltpu.make_async_remote_copy(
                src_ref=src_of(peer), dst_ref=dst,
                send_sem=mem_send.at[kind, t], recv_sem=mem_recv.at[kind, t],
                device_id={"mem": peer}, device_id_type=MESH))
        return made

    xrims = [rim_copy(0, d, xall, OFF_C, xstage, xall) for d in range(8)]
    erims = [rim_copy(1, d, eall, OFF_C, estage, eall) for d in range(8)]
    arims = [rim_copy(2, d, azs, 0, astage, aall) for d in range(8)]
    ccopies = mem_copies(0, lambda peer: colall.at[me], colall.at[me])
    gcopies = mem_copies(1, lambda peer: gsend.at[rows_of(peer), :], grecv.at[mine, :])
    rcopies = mem_copies(2, lambda peer: rall.at[mine, :], rall.at[mine, :])

    for c in ccopies:
        c.start()
    start_rims(xrims)

    for c in loads_e:
        c.wait()
    field = eall[OFF_C:OFF_C + CELLS, :].astype(f32).reshape(TILE, TILE, WIDE)
    for dz, dl, row, rows in REGIONS[2:]:
        estage[row - OFF_L:row - OFF_L + rows, :] = piece(dz, dl, field).astype(bf16)
    start_some(erims, range(8), False)

    shift = iota((32, 48), 1) - iota((32, 48), 0)
    for index, (tap, coord) in enumerate(zip((tlon, tlat), column_coords())):
        here = jnp.where(iota((48, EXT), 0) == jnp.broadcast_to(coord, (48, EXT)), 1.0, 0.0).astype(bf16)
        ahead = jnp.zeros((32, 48), f32)
        back = jnp.zeros((32, 48), f32)
        for k in range(TAPS):
            ahead = jnp.where(shift == k, tap[k], ahead)
            back = jnp.where(shift == k, tap[TAPS - 1 - k], back)
        if index == 1:
            back = -descent * back
        back = back.astype(bf16)
        tabs[index] = dot(ahead.astype(bf16), here).astype(bf16)
        tabs[2 + index, :, 0:PAD_C] = dot(back, here[:, OFF_C:EXT]).astype(bf16)
        for d in range(8):
            n = REGIONS[d][3]
            coord = region_coords(d, n)[index]
            rim = jnp.where(iota((48, n), 0) == jnp.broadcast_to(coord, (48, n)), 1.0, 0.0).astype(bf16)
            back_tabs[index, d, :, 0:n] = dot(back, rim).astype(bf16)

    quality = jnp.zeros((SLOTS, LEV), f32)
    slot = iota((SLOTS, LEV), 0)
    for s in range(SLOTS):
        quality = jnp.where(slot == s, qual[0, 0, 0, s].astype(f32), quality)
    weights = jnp.where(slot < count[0, 0, 0], 0.5 * quality, 0.0)

    for c in ccopies:
        c.wait_recv()
    total = n_mem * SLOTS
    table_i, table_j = by_tile(jnp.concatenate([colall[o] for o in range(n_mem)], axis=0))
    row = iota((total, LEV), 0)
    spread_rows = one_hot(iota((total, 1), 0) >> 4, n_mem)
    lane = iota((total, LEV), 1)
    own_slot = lane == (row & 15)

    def along_rows(table):
        wide = dot(spread_rows, table.astype(f32).astype(bf16))
        return jnp.sum(jnp.where(own_slot, wide, 0.0), axis=1, keepdims=True)

    own_i, own_j = along_rows(table_i), along_rows(table_j)
    lanes = iota((total, 32), 1).astype(f32)
    pick_i = jnp.where(lanes == own_i, 1.0, 0.0).astype(bf16)
    pick_j = jnp.where(lanes == own_j, 1.0, 0.0).astype(bf16)
    for q in range(0, EXT, 128):
        part = dot(pick_i, tabs[0, :, q:q + 128]) * dot(pick_j, tabs[1, :, q:q + 128])
        w2[:, q:q + 128] = part.astype(bf16)

    acc[...] = dot(w2[:, OFF_C:EXT], xall[OFF_C:EXT, :])
    column = jnp.broadcast_to(TILE * own_i + own_j, (total, LEV))
    lane = lane.astype(f32)
    select = jnp.concatenate(
        [jnp.where(lane + float(q) == column, 1.0, 0.0).astype(bf16) for q in range(0, PAD_C, 128)], axis=1)
    ensobs[...] = dot(select, eall[OFF_C:EXT, :])
    for lo, hi, row, rows in GROUPS:
        recv_rims(xrims, lo, hi)
        acc[...] += dot(w2[:, row:row + rows], xall[row:row + rows, :])
    product = acc[...] * ensobs[...]
    part = product[:, 0:LEV]
    for m in range(1, MEM):
        part = part + product[:, m * LEV:(m + 1) * LEV]
    gsend[...] = part.astype(bf16)
    for c in gcopies:
        c.start()
    start_some(erims, (2, 3), True)
    grecv[mine, :] = gsend[mine, :]

    column_t = jnp.transpose(column)[0:1, :]
    cell = iota((CELLS, total), 0).astype(f32)
    st[...] = jnp.where(cell == jnp.broadcast_to(column_t, (CELLS, total)), 1.0, 0.0).astype(bf16)

    def build(b, _):
        rows = pl.ds(pl.multiple_of(b * 64, 64), 64)
        i, j = by_tile(iota((64, 1), 0) + b * 64)
        at_i, at_j = one_hot(i, 32), one_hot(j, 32)
        for q in range(0, PAD_C, 128):
            part = dot(at_i, tabs[2, :, q:q + 128]) * dot(at_j, tabs[3, :, q:q + 128])
            k2c[rows, q:q + 128] = part.astype(bf16)
        return 0
    lax.fori_loop(0, CELLS // 64, build, 0)
    for d in range(8):
        dz, dl, _, rows = REGIONS[d]
        r = iota((rows, 1), 0)
        i, j = by_tile(r) if dl == 0 else (r >> 3, r & 7)
        i, j = i + (TILE - HALF if dz == 1 else 0), j + (TILE - HALF if dl == 1 else 0)
        part = dot(one_hot(i, 32), back_tabs[0, d, :, 0:rows]) * dot(one_hot(j, 32), back_tabs[1, d, :, 0:rows])
        (k2z, k2l, k2x, k2x)[d // 2][d % 2 if d < 4 else d - 4] = part.astype(bf16)

    for c in gcopies:
        c.wait_recv()
    observed = jnp.zeros((SLOTS, LEV), f32)
    for o in range(n_mem):
        observed = observed + grecv[o * SLOTS:(o + 1) * SLOTS, :].astype(f32)
    residual = weights * (observed - vals[...])
    rall[mine, :] = residual.astype(bf16)
    for c in rcopies:
        c.start()
    start_some(erims, (4, 5, 6, 7), True)
    res_ref[...] = residual
    for m in range(MEM):
        out_ref[m] = (1.0 - descent) * ctrl[:, m * LEV:(m + 1) * LEV].reshape(TILE, TILE, LEV)
    for c in rcopies:
        c.wait_recv()

    adjoint = dot(st[...], rall[...])
    azs[...] = adjoint.astype(bf16)
    field = adjoint.reshape(TILE, TILE, LEV)
    for dz, dl, row, rows in REGIONS[2:]:
        astage[row - OFF_L:row - OFF_L + rows, :] = piece(dz, dl, field).astype(bf16)
    start_rims(arims)

    def weighted(row, rows, adj):
        wide = jnp.concatenate([adj] * MEM, axis=1)
        return (eall[row:row + rows, :].astype(f32) * wide).astype(bf16)

    zero = jnp.zeros((PAD_C - CELLS, LEV), f32)
    back = dot(k2c[...], weighted(OFF_C, PAD_C, jnp.concatenate([adjoint, zero], axis=0)))
    for m in range(MEM):
        out_ref[m] += back[:, m * LEV:(m + 1) * LEV].reshape(TILE, TILE, LEV)
    recv_rims(erims, 0, 8)
    for d in range(8):
        recv_rims(arims, d, d + 1)
        row, rows = REGIONS[d][2:]
        matrix = (k2z, k2l, k2x, k2x)[d // 2][d % 2 if d < 4 else d - 4]
        back = dot(matrix, weighted(row, rows, aall[row:row + rows, :].astype(f32)))
        for m in range(MEM):
            block = block_of(out_ref, m, d)
            block[...] += back[:, m * LEV:(m + 1) * LEV].reshape(block.shape)

    for copies in (xrims, erims, arims):
        sent_rims(copies)
    for copies in (ccopies, gcopies, rcopies):
        for c in copies:
            c.wait_send()


def write(a_ref, b_ref, a_out, b_out, sem):
    copies = [pltpu.make_async_copy(a_ref, a_out, sem.at[0]), pltpu.make_async_copy(b_ref, b_out, sem.at[1])]
    for c in copies:
        c.start()
    for c in copies:
        c.wait()


def shards(sizes, controls, ensemble, taps_lon, taps_lat, obs_columns, obs_count, obs_quality, obs_values):
    n_mem = sizes[2]
    total = n_mem * SLOTS
    vmem = pl.BlockSpec(memory_space=pltpu.VMEM)
    hbm = pl.BlockSpec(memory_space=pltpu.HBM)
    shapes = (jax.ShapeDtypeStruct((MEM, TILE, TILE, LEV), f32), jax.ShapeDtypeStruct((SLOTS, LEV), f32))
    results = pl.pallas_call(
        functools.partial(kernel, sizes),
        out_shape=shapes,
        in_specs=[hbm] * 5 + [pl.BlockSpec(memory_space=pltpu.SMEM)] + [hbm] * 2,
        out_specs=(vmem, vmem),
        scratch_shapes=[
            pltpu.VMEM((CELLS, WIDE), f32),
            pltpu.VMEM((EXT, WIDE), bf16),
            pltpu.VMEM((EXT, WIDE), bf16),
            pltpu.VMEM((EXT, LEV), bf16),
            pltpu.VMEM((OFF_C - OFF_L, WIDE), bf16),
            pltpu.VMEM((OFF_C - OFF_L, WIDE), bf16),
            pltpu.VMEM((CELLS, LEV), bf16),
            pltpu.VMEM((OFF_C - OFF_L, LEV), bf16),
            pltpu.VMEM((n_mem, 1, LEV), jnp.int32),
            pltpu.VMEM((total, LEV), bf16),
            pltpu.VMEM((total, LEV), bf16),
            pltpu.VMEM((total, LEV), bf16),
            pltpu.VMEM((total, EXT), bf16),
            pltpu.VMEM((CELLS, PAD_C), bf16),
            pltpu.VMEM((2, SIDE, SIDE), bf16),
            pltpu.VMEM((2, SIDE, SIDE), bf16),
            pltpu.VMEM((4, CORNER, CORNER), bf16),
            pltpu.VMEM((CELLS, total), bf16),
            pltpu.VMEM((4, 32, EXT), bf16),
            pltpu.VMEM((2, 8, 32, SIDE), bf16),
            pltpu.VMEM((total, WIDE), f32),
            pltpu.VMEM((total, WIDE), f32),
            pltpu.SMEM((TAPS,), f32),
            pltpu.SMEM((TAPS,), f32),
            pltpu.SMEM((1, 1, 1, SLOTS), jnp.int32),
            pltpu.SMEM((1, 1, 1, SLOTS), jnp.int32),
            pltpu.VMEM((SLOTS, LEV), f32),
            pltpu.SemaphoreType.DMA((2 * MEM,)),
            pltpu.SemaphoreType.DMA((5,)),
            pltpu.SemaphoreType.DMA((3, 8)),
            pltpu.SemaphoreType.DMA((3, 8)),
            pltpu.SemaphoreType.DMA((3, n_mem)),
            pltpu.SemaphoreType.DMA((3, n_mem)),
        ],
        compiler_params=pltpu.CompilerParams(collective_id=0, has_side_effects=True, vmem_limit_bytes=30 * 1024 * 1024),
        name="step",
    )(*[x if x.size == 1 else pltpu.with_memory_space_constraint(x, pltpu.HBM) for x in (
        controls.reshape(MEM, CELLS, LEV),
        ensemble.reshape(MEM, CELLS, LEV),
        taps_lon,
        taps_lat,
        obs_columns,
        obs_count,
        obs_quality,
        obs_values.reshape(SLOTS, LEV),
    )])
    new_controls, residual = pl.pallas_call(
        write,
        out_shape=shapes,
        in_specs=[pl.BlockSpec(memory_space=pl.ANY)] * 2,
        out_specs=(hbm, hbm),
        scratch_shapes=[pltpu.SemaphoreType.DMA((2,))],
        compiler_params=pltpu.CompilerParams(vmem_limit_bytes=1 << 20),
        name="write",
    )(*results)
    return new_controls, residual.reshape(obs_values.shape)


def solution(mesh):
    sizes = (mesh.shape["lon"], mesh.shape["lat"], mesh.shape["mem"])
    placed = (
        P("mem", "lon", "lat", None),
        P("mem", "lon", "lat", None),
        P(),
        P(),
        P("lon", "lat", "mem", None),
        P("lon", "lat", "mem"),
        P("lon", "lat", "mem", None),
        P("lon", "lat", "mem", None, None),
    )
    return jax.shard_map(
        functools.partial(shards, sizes),
        mesh=mesh,
        in_specs=placed,
        out_specs=(P("mem", "lon", "lat", None), P("lon", "lat", "mem", None, None)),
        check_vma=False,
    )
```

```python
import functools

import jax
import jax.numpy as jnp
from jax import lax
from jax.experimental import pallas as pl
from jax.experimental.pallas import tpu as pltpu
from jax.sharding import PartitionSpec as P

LEV = 128
TILE = 24
HALF = 8
TAPS = 17
SLOTS = 16
MEM = 4
WIDE = MEM * LEV
CELLS = TILE * TILE
SIDE = TILE * HALF
CORNER = HALF * HALF
descent = 0.5
OFF_Z = 0
OFF_L = 2 * SIDE
OFF_X = 4 * SIDE
OFF_C = 4 * SIDE + 4 * CORNER
EXT = OFF_C + CELLS + 64
PAD_C = CELLS + 64
REGIONS = (
    (-1, 0, OFF_Z, SIDE),
    (1, 0, OFF_Z + SIDE, SIDE),
    (0, -1, OFF_L, SIDE),
    (0, 1, OFF_L + SIDE, SIDE),
    (-1, -1, OFF_X, CORNER),
    (1, -1, OFF_X + CORNER, CORNER),
    (-1, 1, OFF_X + 2 * CORNER, CORNER),
    (1, 1, OFF_X + 3 * CORNER, CORNER),
)
GROUPS = (((2, 3), OFF_L, 2 * SIDE), ((10, 11), OFF_Z, 2 * SIDE), ((4, 5, 6, 7), OFF_X, 4 * CORNER))
MESH = pl.DeviceIdType.MESH
f32 = jnp.float32
bf16 = jnp.bfloat16


def iota(shape, dim):
    return lax.broadcasted_iota(jnp.int32, shape, dim)


def by_tile(q):
    i = (q * 2731) >> 16
    return i, q - TILE * i


def strips(q):
    strip = q >> 6
    first = jnp.where(strip == 0, 0, jnp.where(strip == 1, TILE - HALF, HALF))
    return (q & 63) >> 3, (q & 7) + first


def column_coords():
    lon, lat = [], []
    def add(i, j):
        lon.append(i)
        lat.append(j)
    for base in (0, HALF + TILE):
        i, j = strips(iota((1, SIDE), 1))
        add(i + base, j + HALF)
    for base in (0, HALF + TILE):
        q = iota((1, SIDE), 1)
        add((q >> 3) + HALF, (q & 7) + base)
    for base_lat in (0, HALF + TILE):
        for base_lon in (0, HALF + TILE):
            q = iota((1, CORNER), 1)
            add((q >> 3) + base_lon, (q & 7) + base_lat)
    i, j = by_tile(iota((1, PAD_C), 1))
    ok = iota((1, PAD_C), 1) < CELLS
    add(jnp.where(ok, i + HALF, -1), jnp.where(ok, j + HALF, -1))
    return jnp.concatenate(lon, axis=1), jnp.concatenate(lat, axis=1)


def dot(a, b):
    return jnp.dot(a, b, preferred_element_type=f32)


def lon_rim(rows):
    field = rows.reshape(HALF, TILE, rows.shape[1])
    parts = [field[:, j:j + HALF, :].reshape(CORNER, rows.shape[1]) for j in (0, TILE - HALF, HALF)]
    return jnp.concatenate(parts, axis=0)


def edge(dz, dl, field):
    i0, ni = {-1: (TILE - HALF, HALF), 1: (0, HALF), 0: (0, TILE)}[dz]
    j0 = {-1: TILE - HALF, 1: 0}[dl]
    return field[i0:i0 + ni, j0:j0 + HALF, :].reshape(ni * HALF, field.shape[2])


def stage_edges(stage, field, which):
    n = field.shape[1]
    for d in which:
        dz, dl, row, rows = REGIONS[d]
        if dl == 0:
            first = CELLS - SIDE if dz == -1 else 0
            value = lon_rim(field[first:first + SIDE, :])
        else:
            value = edge(dz, dl, field.reshape(TILE, TILE, n))
        stage[row:row + rows, :] = value.astype(bf16)


def region_coords(d, n):
    dz, dl, _, _ = REGIONS[d]
    start = {-1: 0, 0: HALF, 1: HALF + TILE}
    q = iota((1, n), 1)
    i, j = strips(q) if dl == 0 else (q >> 3, q & 7)
    return i + start[dz], j + start[dl]


def block_of(ref, m, d):
    dz, dl, _, _ = REGIONS[d]
    part = {-1: slice(0, HALF), 0: slice(0, TILE), 1: slice(TILE - HALF, TILE)}
    return ref.at[m, part[dz], part[dl], :]


def one_hot(index, n):
    return jnp.where(iota((index.shape[0], n), 1) == index, 1.0, 0.0).astype(bf16)


def kernel(sizes, ctrl_hbm, ens_hbm, tlon_hbm, tlat_hbm, cols_hbm, count, qual_hbm, vals_hbm, out_ref, res_ref,
           ctrl, xall, eall, aall, xstage, estage, astage, colall, gsend, grecv, rall, w2, k2c, k2z, k2l, k2x, st, tabs,
           back_tabs, ensobs, acc, tlon, tlat, cols, qual, vals,
           load_sem, small_sem, rim_send, rim_recv, mem_send, mem_recv, far_sem):
    n_lon, n_lat, n_mem = sizes
    n_y = n_mem // 2
    z = lax.axis_index("lon")
    l = lax.axis_index("lat")
    me = lax.axis_index("mem")
    my_x, my_y = me // n_y, lax.rem(me, n_y)

    def lon_of(dz):
        return lax.rem(z + dz + n_lon, n_lon)

    def has(dl):
        if dl == 0:
            return None
        return (l + dl >= 0) & (l + dl < n_lat)

    def guarded(cond, f):
        if cond is None:
            f()
        else:
            pl.when(cond)(f)

    steps = [(dx, dy) for dy in sorted(range(n_y), key=lambda y: -min(y, n_y - y)) for dx in (1, 0)]
    steps = [s for s in steps if s != (0, 0)]

    def peer_of(dx, dy):
        return lax.rem(my_x + dx, 2) * n_y + lax.rem(my_y + dy, n_y)

    barrier = pltpu.get_barrier_semaphore()
    near = [(dx, dy) for dx, dy in steps if min(dy, n_y - dy) <= 2]
    for dx, dy in near:
        pl.semaphore_signal(barrier, inc=1, device_id={"mem": peer_of(dx, dy)}, device_id_type=MESH)
    for dz, dl, _, _ in REGIONS:
        def greet(dz=dz, dl=dl):
            pl.semaphore_signal(barrier, inc=1, device_id={"lon": lon_of(dz), "lat": l + dl}, device_id_type=MESH)
        guarded(has(dl), greet)

    loads = []
    for part, first in enumerate((0, CELLS - SIDE, SIDE)):
        loads.append([
            pltpu.make_async_copy(
                ctrl_hbm.at[m, first:first + SIDE, :], ctrl.at[first:first + SIDE, m * LEV:(m + 1) * LEV], load_sem.at[part, m])
            for m in range(MEM)
        ])
    loads_e = [
        pltpu.make_async_copy(ens_hbm.at[m], eall.at[OFF_C:OFF_C + CELLS, m * LEV:(m + 1) * LEV], load_sem.at[3, m])
        for m in range(MEM)
    ]
    pairs = ((cols_hbm, cols), (qual_hbm, qual), (tlon_hbm, tlon), (tlat_hbm, tlat), (vals_hbm, vals))
    small = [pltpu.make_async_copy(a, b, small_sem.at[k]) for k, (a, b) in enumerate(pairs)]
    for c in loads[0] + loads[1] + loads[2] + small + loads_e:
        c.start()

    xall[OFF_C + CELLS:EXT, :] = jnp.zeros((64, WIDE), bf16)
    eall[OFF_C + CELLS:EXT, :] = jnp.zeros((64, WIDE), bf16)
    for dl, row, xrow in ((-1, OFF_L, OFF_X), (1, OFF_L + SIDE, OFF_X + 2 * CORNER)):
        @pl.when(jnp.logical_not(has(dl)))
        def _(row=row, xrow=xrow):
            for ref in (xall, eall):
                ref[row:row + SIDE, :] = jnp.zeros((SIDE, WIDE), bf16)
                ref[xrow:xrow + 2 * CORNER, :] = jnp.zeros((2 * CORNER, WIDE), bf16)
            aall[row:row + SIDE, :] = jnp.zeros((SIDE, LEV), bf16)
            aall[xrow:xrow + 2 * CORNER, :] = jnp.zeros((2 * CORNER, LEV), bf16)

    for part, (dz, dl, row, rows) in ((1, REGIONS[0]), (0, REGIONS[1])):
        for c in loads[part]:
            c.wait()
        first = CELLS - SIDE if dz == -1 else 0
        xstage[row:row + rows, :] = lon_rim(ctrl[first:first + SIDE, :]).astype(bf16)

    for c in small:
        c.wait()
    lane1 = iota((1, LEV), 1)
    col = jnp.zeros((1, LEV), jnp.int32)
    for s in range(SLOTS):
        col = jnp.where(lane1 == s, cols[0, 0, 0, s], col)
    colall[me] = col

    around = jnp.where((l > 0) & (l < n_lat - 1), 8, 5)
    pl.semaphore_wait(barrier, around + len(near))

    def rim_copy(kind, d, lo, hi, src, dst, sem, dz, dl):
        row = REGIONS[d][2]
        return pltpu.make_async_remote_copy(
            src_ref=src, dst_ref=dst.at[row + lo:row + hi, :],
            send_sem=rim_send.at[kind, sem], recv_sem=rim_recv.at[kind, sem],
            device_id={"lon": lon_of(-dz), "lat": l - dl}, device_id_type=MESH)

    def rim_copies(kind, stage, dst):
        made = []
        for sem in range(12):
            d = sem if sem < 8 else sem % 2
            dz, dl, row, rows = REGIONS[d]
            lo, hi = (CORNER * (max(sem - 6, 0) // 2), CORNER * (max(sem - 6, 0) // 2 + 1)) if d < 2 else (0, rows)
            if d < 4:
                src = stage.at[row + lo:row + hi, :]
            else:
                first = (OFF_Z if dz == -1 else OFF_Z + SIDE) + (CORNER if dl == -1 else 0)
                src, dz = dst.at[first:first + CORNER, :], 0
            made.append(rim_copy(kind, d, lo, hi, src, dst, sem, dz, dl))
        return made

    def adjoint_copies(stage, dst):
        made = []
        for d, (dz, dl, row, rows) in enumerate(REGIONS):
            made.append(rim_copy(2, d, 0, rows, stage.at[row:row + rows, :], dst, d, dz, dl))
        return made

    def crosses(d):
        return lax.rem(l, 2) == (1 if REGIONS[d][1] == -1 else 0)

    def lat_of(sem):
        return REGIONS[sem][1] if sem < 8 else 0

    def start_rims(copies, which):
        for d in which:
            guarded(has(-lat_of(d)), copies[d].start)

    def start_some(copies, which, across):
        for d in which:
            dl = REGIONS[d][1]
            if dl == 0:
                if not across:
                    copies[d].start()
            else:
                far = crosses(d)
                guarded(has(-dl) & (far if across else jnp.logical_not(far)), copies[d].start)

    def recv_rims(copies, which):
        for d in which:
            guarded(has(lat_of(d)), copies[d].wait_recv)

    def sent_rims(copies):
        for d, c in enumerate(copies):
            guarded(has(-lat_of(d)), c.wait_send)

    def by_parity(odd, even):
        pl.when(lax.rem(l, 2) == 1)(odd)
        pl.when(lax.rem(l, 2) == 0)(even)

    def send_strips(copies):
        by_parity(lambda: start_rims(copies, (0, 1, 8, 9)), lambda: start_rims(copies, (8, 9, 0, 1)))

    def pass_strips(copies, across):
        def high(start):
            recv_rims(copies, (8, 9))
            if start:
                start_rims(copies, (4, 5))

        def low(start):
            recv_rims(copies, (0, 1))
            if start:
                start_rims(copies, (6, 7))

        def low_high():
            low(True)
            high(across)

        def high_low():
            high(True)
            low(across)

        by_parity(low_high, high_low)

    def rows_of(index):
        return pl.ds(pl.multiple_of(index * SLOTS, SLOTS), SLOTS)

    mine = rows_of(me)

    def mem_copies(kind, src_of, dst):
        made = []
        for t, (dx, dy) in enumerate(steps):
            peer = peer_of(dx, dy)
            made.append(pltpu.make_async_remote_copy(
                src_ref=src_of(peer), dst_ref=dst,
                send_sem=mem_send.at[kind, t], recv_sem=mem_recv.at[kind, t],
                device_id={"mem": peer}, device_id_type=MESH))
        return made

    xrims = rim_copies(0, xstage, xall)
    erims = rim_copies(1, estage, eall)
    arims = adjoint_copies(astage, aall)
    ccopies = mem_copies(0, lambda peer: colall.at[me], colall.at[me])
    gcopies = mem_copies(1, lambda peer: gsend.at[rows_of(peer), :], grecv.at[mine, :])
    rcopies = mem_copies(2, lambda peer: rall.at[mine, :], rall.at[mine, :])

    far = [(0, 2), (0, n_y - 2)] if len(near) < len(steps) else []
    for dx, dy in far:
        pl.semaphore_signal(far_sem, inc=1, device_id={"mem": peer_of(dx, dy)}, device_id_type=MESH)
    for d in range(4, 8):
        dz, dl, row, rows = REGIONS[d]
        first = (OFF_Z if dz == -1 else OFF_Z + SIDE) + (CORNER if dl == -1 else 0)
        corner = rim_copy(0, d, 0, rows, xstage.at[first:first + rows, :], xall, d, dz, dl)
        guarded(has(-dl) & crosses(d), corner.start)
    send_strips(xrims)
    start_rims(xrims, (10, 11))
    for c in loads[2]:
        c.wait()
    stage_edges(xstage, ctrl[...], (2, 3))
    start_rims(xrims, (2, 3))

    shift = iota((32, 48), 1) - iota((32, 48), 0)
    for index, (tap, coord) in enumerate(zip((tlon, tlat), column_coords())):
        here = jnp.where(iota((48, EXT), 0) == jnp.broadcast_to(coord, (48, EXT)), 1.0, 0.0).astype(bf16)
        ahead = jnp.zeros((32, 48), f32)
        back = jnp.zeros((32, 48), f32)
        for k in range(TAPS):
            ahead = jnp.where(shift == k, tap[k], ahead)
            back = jnp.where(shift == k, tap[TAPS - 1 - k], back)
        if index == 1:
            back = -descent * back
        back = back.astype(bf16)
        tabs[index] = dot(ahead.astype(bf16), here).astype(bf16)
        tabs[2 + index, :, 0:PAD_C] = dot(back, here[:, OFF_C:EXT]).astype(bf16)
        for d in range(8):
            n = REGIONS[d][3]
            coord = region_coords(d, n)[index]
            rim = jnp.where(iota((48, n), 0) == jnp.broadcast_to(coord, (48, n)), 1.0, 0.0).astype(bf16)
            back_tabs[index, d, :, 0:n] = dot(back, rim).astype(bf16)

    if far:
        pl.semaphore_wait(far_sem, len(far))
    for c in ccopies:
        c.start()
    pass_strips(xrims, False)
    for c in loads_e:
        c.wait()
    stage_edges(estage, eall[OFF_C:OFF_C + CELLS, :].astype(f32), range(4))
    start_rims(erims, (0, 1, 8, 9, 10, 11))
    start_some(erims, (2, 3), False)
    xall[OFF_C:OFF_C + CELLS, :] = ctrl[...].astype(bf16)

    quality = jnp.zeros((SLOTS, LEV), f32)
    slot = iota((SLOTS, LEV), 0)
    for s in range(SLOTS):
        quality = jnp.where(slot == s, qual[0, 0, 0, s].astype(f32), quality)
    weights = jnp.where(slot < count[0, 0, 0], 0.5 * quality, 0.0)

    for c in ccopies:
        c.wait_recv()
    total = n_mem * SLOTS
    table_i, table_j = by_tile(jnp.concatenate([colall[o] for o in range(n_mem)], axis=0))
    row = iota((total, LEV), 0)
    spread_rows = one_hot(iota((total, 1), 0) >> 4, n_mem)
    lane = iota((total, LEV), 1)
    own_slot = lane == (row & 15)

    def along_rows(table):
        wide = dot(spread_rows, table.astype(f32).astype(bf16))
        return jnp.sum(jnp.where(own_slot, wide, 0.0), axis=1, keepdims=True)

    own_i, own_j = along_rows(table_i), along_rows(table_j)
    lanes = iota((total, 32), 1).astype(f32)
    pick_i = jnp.where(lanes == own_i, 1.0, 0.0).astype(bf16)
    pick_j = jnp.where(lanes == own_j, 1.0, 0.0).astype(bf16)
    for q in range(0, EXT, 128):
        part = dot(pick_i, tabs[0, :, q:q + 128]) * dot(pick_j, tabs[1, :, q:q + 128])
        w2[:, q:q + 128] = part.astype(bf16)

    acc[...] = dot(w2[:, OFF_C:EXT], xall[OFF_C:EXT, :])
    column = jnp.broadcast_to(TILE * own_i + own_j, (total, LEV))
    lane = lane.astype(f32)
    select = jnp.concatenate(
        [jnp.where(lane + float(q) == column, 1.0, 0.0).astype(bf16) for q in range(0, PAD_C, 128)], axis=1)
    ensobs[...] = dot(select, eall[OFF_C:EXT, :])
    for which, row, rows in GROUPS:
        recv_rims(xrims, which)
        acc[...] += dot(w2[:, row:row + rows], xall[row:row + rows, :])
    product = acc[...] * ensobs[...]
    part = product[:, 0:LEV]
    for m in range(1, MEM):
        part = part + product[:, m * LEV:(m + 1) * LEV]
    gsend[...] = part.astype(bf16)
    for c in gcopies:
        c.start()
    start_some(erims, (2, 3), True)
    grecv[mine, :] = gsend[mine, :]

    column_t = jnp.transpose(column)[0:1, :]
    cell = iota((CELLS, total), 0).astype(f32)
    st[...] = jnp.where(cell == jnp.broadcast_to(column_t, (CELLS, total)), 1.0, 0.0).astype(bf16)

    def build(b, _):
        rows = pl.ds(pl.multiple_of(b * 64, 64), 64)
        i, j = by_tile(iota((64, 1), 0) + b * 64)
        at_i, at_j = one_hot(i, 32), one_hot(j, 32)
        for q in range(0, PAD_C, 128):
            part = dot(at_i, tabs[2, :, q:q + 128]) * dot(at_j, tabs[3, :, q:q + 128])
            k2c[rows, q:q + 128] = part.astype(bf16)
        return 0
    lax.fori_loop(0, CELLS // 64, build, 0)
    for d in range(8):
        dz, dl, _, rows = REGIONS[d]
        r = iota((rows, 1), 0)
        i, j = by_tile(r) if dl == 0 else (r >> 3, r & 7)
        i, j = i + (TILE - HALF if dz == 1 else 0), j + (TILE - HALF if dl == 1 else 0)
        part = dot(one_hot(i, 32), back_tabs[0, d, :, 0:rows]) * dot(one_hot(j, 32), back_tabs[1, d, :, 0:rows])
        (k2z, k2l, k2x, k2x)[d // 2][d % 2 if d < 4 else d - 4] = part.astype(bf16)

    for c in gcopies:
        c.wait_recv()
    observed = jnp.zeros((SLOTS, LEV), f32)
    for o in range(n_mem):
        observed = observed + grecv[o * SLOTS:(o + 1) * SLOTS, :].astype(f32)
    residual = weights * (observed - vals[...])
    rall[mine, :] = residual.astype(bf16)
    for c in rcopies:
        c.start()
    pass_strips(erims, True)
    res_ref[...] = residual
    for m in range(MEM):
        out_ref[m] = (1.0 - descent) * ctrl[:, m * LEV:(m + 1) * LEV].reshape(TILE, TILE, LEV)
    sent_rims(xrims)
    for c in ccopies + gcopies:
        c.wait_send()
    for c in rcopies:
        c.wait_recv()

    adjoint = dot(st[...], rall[...])
    stage_edges(astage, adjoint, range(8))
    start_rims(arims, (4, 5, 6, 7, 2, 3, 0, 1))

    zero = jnp.zeros((PAD_C - CELLS, LEV), f32)
    wide = jnp.concatenate([jnp.concatenate([adjoint, zero], axis=0)] * MEM, axis=1)
    back = dot(k2c[...], (eall[OFF_C:EXT, :].astype(f32) * wide).astype(bf16))
    for m in range(MEM):
        out_ref[m] += back[:, m * LEV:(m + 1) * LEV].reshape(TILE, TILE, LEV)
    recv_rims(erims, (2, 3, 4, 5, 6, 7, 10, 11))
    sent_rims(erims)
    for c in rcopies:
        c.wait_send()
    for d in (2, 3, 0, 1, 4, 5, 6, 7):
        recv_rims(arims, (d,))
        row, rows = REGIONS[d][2:]
        matrix = (k2z, k2l, k2x, k2x)[d // 2][d % 2 if d < 4 else d - 4]
        back = dot(matrix, eall[row:row + rows, :] * jnp.concatenate([aall[row:row + rows, :]] * MEM, axis=1))
        for m in range(MEM):
            block = block_of(out_ref, m, d)
            block[...] += back[:, m * LEV:(m + 1) * LEV].reshape(block.shape)

    sent_rims(arims)


def write(a_ref, b_ref, a_out, b_out, sem):
    copies = [pltpu.make_async_copy(a_ref, a_out, sem.at[0]), pltpu.make_async_copy(b_ref, b_out, sem.at[1])]
    for c in copies:
        c.start()
    for c in copies:
        c.wait()


def shards(sizes, controls, ensemble, taps_lon, taps_lat, obs_columns, obs_count, obs_quality, obs_values):
    n_mem = sizes[2]
    total = n_mem * SLOTS
    vmem = pl.BlockSpec(memory_space=pltpu.VMEM)
    hbm = pl.BlockSpec(memory_space=pltpu.HBM)
    shapes = (jax.ShapeDtypeStruct((MEM, TILE, TILE, LEV), f32), jax.ShapeDtypeStruct((SLOTS, LEV), f32))
    results = pl.pallas_call(
        functools.partial(kernel, sizes),
        out_shape=shapes,
        in_specs=[hbm] * 5 + [pl.BlockSpec(memory_space=pltpu.SMEM)] + [hbm] * 2,
        out_specs=(vmem, vmem),
        scratch_shapes=[
            pltpu.VMEM((CELLS, WIDE), f32),
            pltpu.VMEM((EXT, WIDE), bf16),
            pltpu.VMEM((EXT, WIDE), bf16),
            pltpu.VMEM((EXT, LEV), bf16),
            pltpu.VMEM((OFF_X, WIDE), bf16),
            pltpu.VMEM((OFF_X, WIDE), bf16),
            pltpu.VMEM((OFF_C, LEV), bf16),
            pltpu.VMEM((n_mem, 1, LEV), jnp.int32),
            pltpu.VMEM((total, LEV), bf16),
            pltpu.VMEM((total, LEV), bf16),
            pltpu.VMEM((total, LEV), bf16),
            pltpu.VMEM((total, EXT), bf16),
            pltpu.VMEM((CELLS, PAD_C), bf16),
            pltpu.VMEM((2, SIDE, SIDE), bf16),
            pltpu.VMEM((2, SIDE, SIDE), bf16),
            pltpu.VMEM((4, CORNER, CORNER), bf16),
            pltpu.VMEM((CELLS, total), bf16),
            pltpu.VMEM((4, 32, EXT), bf16),
            pltpu.VMEM((2, 8, 32, SIDE), bf16),
            pltpu.VMEM((total, WIDE), f32),
            pltpu.VMEM((total, WIDE), f32),
            pltpu.SMEM((TAPS,), f32),
            pltpu.SMEM((TAPS,), f32),
            pltpu.SMEM((1, 1, 1, SLOTS), jnp.int32),
            pltpu.SMEM((1, 1, 1, SLOTS), jnp.int32),
            pltpu.VMEM((SLOTS, LEV), f32),
            pltpu.SemaphoreType.DMA((4, MEM)),
            pltpu.SemaphoreType.DMA((5,)),
            pltpu.SemaphoreType.DMA((3, 12)),
            pltpu.SemaphoreType.DMA((3, 12)),
            pltpu.SemaphoreType.DMA((3, n_mem)),
            pltpu.SemaphoreType.DMA((3, n_mem)),
            pltpu.SemaphoreType.REGULAR,
        ],
        compiler_params=pltpu.CompilerParams(collective_id=0, has_side_effects=True, vmem_limit_bytes=30 * 1024 * 1024),
        name="step",
    )(*[x if x.size == 1 else pltpu.with_memory_space_constraint(x, pltpu.HBM) for x in (
        controls.reshape(MEM, CELLS, LEV),
        ensemble.reshape(MEM, CELLS, LEV),
        taps_lon,
        taps_lat,
        obs_columns,
        obs_count,
        obs_quality,
        obs_values.reshape(SLOTS, LEV),
    )])
    new_controls, residual = pl.pallas_call(
        write,
        out_shape=shapes,
        in_specs=[pl.BlockSpec(memory_space=pl.ANY)] * 2,
        out_specs=(hbm, hbm),
        scratch_shapes=[pltpu.SemaphoreType.DMA((2,))],
        compiler_params=pltpu.CompilerParams(vmem_limit_bytes=1 << 20),
        name="write",
    )(*results)
    return new_controls, residual.reshape(obs_values.shape)


def solution(mesh):
    sizes = (mesh.shape["lon"], mesh.shape["lat"], mesh.shape["mem"])
    placed = (
        P("mem", "lon", "lat", None),
        P("mem", "lon", "lat", None),
        P(),
        P(),
        P("lon", "lat", "mem", None),
        P("lon", "lat", "mem"),
        P("lon", "lat", "mem", None),
        P("lon", "lat", "mem", None, None),
    )
    return jax.shard_map(
        functools.partial(shards, sizes),
        mesh=mesh,
        in_specs=placed,
        out_specs=(P("mem", "lon", "lat", None), P("lon", "lat", "mem", None, None)),
        check_vma=False,
    )
```

```python
import functools

import jax
import jax.numpy as jnp
from jax import lax
from jax.experimental import pallas as pl
from jax.experimental.pallas import tpu as pltpu
from jax.sharding import PartitionSpec as P

LEV = 128
TILE = 24
HALF = 8
TAPS = 17
SLOTS = 16
MEM = 4
WIDE = MEM * LEV
CELLS = TILE * TILE
SIDE = TILE * HALF
CORNER = HALF * HALF
descent = 0.5
OFF_Z = 0
OFF_L = 2 * SIDE
OFF_X = 4 * SIDE
OFF_C = 4 * SIDE + 4 * CORNER
EXT = OFF_C + CELLS + 64
PAD_C = CELLS + 64
REGIONS = (
    (-1, 0, OFF_Z, SIDE),
    (1, 0, OFF_Z + SIDE, SIDE),
    (0, -1, OFF_L, SIDE),
    (0, 1, OFF_L + SIDE, SIDE),
    (-1, -1, OFF_X, CORNER),
    (1, -1, OFF_X + CORNER, CORNER),
    (-1, 1, OFF_X + 2 * CORNER, CORNER),
    (1, 1, OFF_X + 3 * CORNER, CORNER),
)
GROUPS = (((2, 3), OFF_L, 2 * SIDE), ((10, 11), OFF_Z, 2 * SIDE), ((4, 5, 6, 7), OFF_X, 4 * CORNER))
MESH = pl.DeviceIdType.MESH
f32 = jnp.float32
bf16 = jnp.bfloat16


def iota(shape, dim):
    return lax.broadcasted_iota(jnp.int32, shape, dim)


def by_tile(q):
    i = (q * 2731) >> 16
    return i, q - TILE * i


def strips(q):
    strip = q >> 6
    first = jnp.where(strip == 0, 0, jnp.where(strip == 1, TILE - HALF, HALF))
    return (q & 63) >> 3, (q & 7) + first


def column_coords():
    lon, lat = [], []
    def add(i, j):
        lon.append(i)
        lat.append(j)
    for base in (0, HALF + TILE):
        i, j = strips(iota((1, SIDE), 1))
        add(i + base, j + HALF)
    for base in (0, HALF + TILE):
        q = iota((1, SIDE), 1)
        add((q >> 3) + HALF, (q & 7) + base)
    for base_lat in (0, HALF + TILE):
        for base_lon in (0, HALF + TILE):
            q = iota((1, CORNER), 1)
            add((q >> 3) + base_lon, (q & 7) + base_lat)
    i, j = by_tile(iota((1, PAD_C), 1))
    ok = iota((1, PAD_C), 1) < CELLS
    add(jnp.where(ok, i + HALF, -1), jnp.where(ok, j + HALF, -1))
    return jnp.concatenate(lon, axis=1), jnp.concatenate(lat, axis=1)


def dot(a, b):
    return jnp.dot(a, b, preferred_element_type=f32)


def lon_rim(rows):
    field = rows.reshape(HALF, TILE, rows.shape[1])
    parts = [field[:, j:j + HALF, :].reshape(CORNER, rows.shape[1]) for j in (0, TILE - HALF, HALF)]
    return jnp.concatenate(parts, axis=0)


def edge(dz, dl, field):
    i0, ni = {-1: (TILE - HALF, HALF), 1: (0, HALF), 0: (0, TILE)}[dz]
    j0 = {-1: TILE - HALF, 1: 0}[dl]
    return field[i0:i0 + ni, j0:j0 + HALF, :].reshape(ni * HALF, field.shape[2])


def stage_edges(stage, field, which):
    n = field.shape[1]
    for d in which:
        dz, dl, row, rows = REGIONS[d]
        if dl == 0:
            first = CELLS - SIDE if dz == -1 else 0
            value = lon_rim(field[first:first + SIDE, :])
        else:
            value = edge(dz, dl, field.reshape(TILE, TILE, n))
        stage[row:row + rows, :] = value.astype(bf16)


def region_coords(d, n):
    dz, dl, _, _ = REGIONS[d]
    start = {-1: 0, 0: HALF, 1: HALF + TILE}
    q = iota((1, n), 1)
    i, j = strips(q) if dl == 0 else (q >> 3, q & 7)
    return i + start[dz], j + start[dl]


def block_of(ref, m, d):
    dz, dl, _, _ = REGIONS[d]
    part = {-1: slice(0, HALF), 0: slice(0, TILE), 1: slice(TILE - HALF, TILE)}
    return ref.at[m, part[dz], part[dl], :]


def one_hot(index, n):
    return jnp.where(iota((index.shape[0], n), 1) == index, 1.0, 0.0).astype(bf16)


def kernel(sizes, ctrl_hbm, ens_hbm, tlon_hbm, tlat_hbm, cols_hbm, count, qual_hbm, vals_hbm, out_ref, res_ref,
           ctrl, xall, eall, aall, xstage, estage, astage, colall, gsend, grecv, rall, w2, k2c, k2z, k2l, k2x, st, tabs,
           back_tabs, ensobs, acc, tlon, tlat, cols, qual, vals,
           load_sem, small_sem, rim_send, rim_recv, mem_send, mem_recv, far_sem):
    n_lon, n_lat, n_mem = sizes
    n_y = n_mem // 2
    z = lax.axis_index("lon")
    l = lax.axis_index("lat")
    me = lax.axis_index("mem")
    my_x, my_y = me // n_y, lax.rem(me, n_y)

    def lon_of(dz):
        return lax.rem(z + dz + n_lon, n_lon)

    def has(dl):
        if dl == 0:
            return None
        return (l + dl >= 0) & (l + dl < n_lat)

    def guarded(cond, f):
        if cond is None:
            f()
        else:
            pl.when(cond)(f)

    steps = [(dx, dy) for dy in sorted(range(n_y), key=lambda y: -min(y, n_y - y)) for dx in (1, 0)]
    steps = [s for s in steps if s != (0, 0)]

    def peer_of(dx, dy):
        return lax.rem(my_x + dx, 2) * n_y + lax.rem(my_y + dy, n_y)

    barrier = pltpu.get_barrier_semaphore()
    near = [(dx, dy) for dx, dy in steps if min(dy, n_y - dy) <= 2]
    for dx, dy in near:
        pl.semaphore_signal(barrier, inc=1, device_id={"mem": peer_of(dx, dy)}, device_id_type=MESH)
    for dz, dl, _, _ in REGIONS:
        def greet(dz=dz, dl=dl):
            pl.semaphore_signal(barrier, inc=1, device_id={"lon": lon_of(dz), "lat": l + dl}, device_id_type=MESH)
        guarded(has(dl), greet)

    loads = []
    for part, first in enumerate((0, CELLS - SIDE, SIDE)):
        loads.append([
            pltpu.make_async_copy(
                ctrl_hbm.at[m, first:first + SIDE, :], ctrl.at[first:first + SIDE, m * LEV:(m + 1) * LEV], load_sem.at[part, m])
            for m in range(MEM)
        ])
    loads_e = [
        pltpu.make_async_copy(ens_hbm.at[m], eall.at[OFF_C:OFF_C + CELLS, m * LEV:(m + 1) * LEV], load_sem.at[3, m])
        for m in range(MEM)
    ]
    pairs = ((cols_hbm, cols), (qual_hbm, qual), (tlon_hbm, tlon), (tlat_hbm, tlat), (vals_hbm, vals))
    small = [pltpu.make_async_copy(a, b, small_sem.at[k]) for k, (a, b) in enumerate(pairs)]
    for c in loads[0] + loads[1] + loads[2] + small + loads_e:
        c.start()

    xall[OFF_C + CELLS:EXT, :] = jnp.zeros((64, WIDE), bf16)
    eall[OFF_C + CELLS:EXT, :] = jnp.zeros((64, WIDE), bf16)
    for dl, row, xrow in ((-1, OFF_L, OFF_X), (1, OFF_L + SIDE, OFF_X + 2 * CORNER)):
        @pl.when(jnp.logical_not(has(dl)))
        def _(row=row, xrow=xrow):
            for ref in (xall, eall):
                ref[row:row + SIDE, :] = jnp.zeros((SIDE, WIDE), bf16)
                ref[xrow:xrow + 2 * CORNER, :] = jnp.zeros((2 * CORNER, WIDE), bf16)
            aall[row:row + SIDE, :] = jnp.zeros((SIDE, LEV), bf16)
            aall[xrow:xrow + 2 * CORNER, :] = jnp.zeros((2 * CORNER, LEV), bf16)

    for part, (dz, dl, row, rows) in ((1, REGIONS[0]), (0, REGIONS[1])):
        for c in loads[part]:
            c.wait()
        first = CELLS - SIDE if dz == -1 else 0
        xstage[row:row + rows, :] = lon_rim(ctrl[first:first + SIDE, :]).astype(bf16)

    for c in small:
        c.wait()
    lane1 = iota((1, LEV), 1)
    col = jnp.zeros((1, LEV), jnp.int32)
    for s in range(SLOTS):
        col = jnp.where(lane1 == s, cols[0, 0, 0, s], col)
    colall[me] = col

    around = jnp.where((l > 0) & (l < n_lat - 1), 8, 5)
    pl.semaphore_wait(barrier, around + len(near))

    def rim_copy(kind, d, lo, hi, src, dst, sem, dz, dl):
        row = REGIONS[d][2]
        return pltpu.make_async_remote_copy(
            src_ref=src, dst_ref=dst.at[row + lo:row + hi, :],
            send_sem=rim_send.at[kind, sem], recv_sem=rim_recv.at[kind, sem],
            device_id={"lon": lon_of(-dz), "lat": l - dl}, device_id_type=MESH)

    def rim_copies(kind, stage, dst):
        made = []
        for sem in range(12):
            d = sem if sem < 8 else sem % 2
            dz, dl, row, rows = REGIONS[d]
            lo, hi = (CORNER * (max(sem - 6, 0) // 2), CORNER * (max(sem - 6, 0) // 2 + 1)) if d < 2 else (0, rows)
            if d < 4:
                src = stage.at[row + lo:row + hi, :]
            else:
                first = (OFF_Z if dz == -1 else OFF_Z + SIDE) + (CORNER if dl == -1 else 0)
                src, dz = dst.at[first:first + CORNER, :], 0
            made.append(rim_copy(kind, d, lo, hi, src, dst, sem, dz, dl))
        return made

    def adjoint_copies(stage, dst):
        made = []
        for d, (dz, dl, row, rows) in enumerate(REGIONS):
            made.append(rim_copy(2, d, 0, rows, stage.at[row:row + rows, :], dst, d, dz, dl))
        return made

    def crosses(d):
        return lax.rem(l, 2) == (1 if REGIONS[d][1] == -1 else 0)

    def lat_of(sem):
        return REGIONS[sem][1] if sem < 8 else 0

    def start_rims(copies, which):
        for d in which:
            guarded(has(-lat_of(d)), copies[d].start)

    def start_some(copies, which, across):
        for d in which:
            dl = REGIONS[d][1]
            if dl == 0:
                if not across:
                    copies[d].start()
            else:
                far = crosses(d)
                guarded(has(-dl) & (far if across else jnp.logical_not(far)), copies[d].start)

    def recv_rims(copies, which):
        for d in which:
            guarded(has(lat_of(d)), copies[d].wait_recv)

    def sent_rims(copies):
        for d, c in enumerate(copies):
            guarded(has(-lat_of(d)), c.wait_send)

    def by_parity(odd, even):
        pl.when(lax.rem(l, 2) == 1)(odd)
        pl.when(lax.rem(l, 2) == 0)(even)

    def send_strips(copies):
        by_parity(lambda: start_rims(copies, (8, 9, 0, 1)), lambda: start_rims(copies, (0, 1, 8, 9)))

    def pass_strips(copies):
        def high():
            recv_rims(copies, (8, 9))
            start_rims(copies, (4, 5))

        def low():
            recv_rims(copies, (0, 1))
            start_rims(copies, (6, 7))

        def high_low():
            high()
            low()

        def low_high():
            low()
            high()

        by_parity(high_low, low_high)

    def rows_of(index):
        return pl.ds(pl.multiple_of(index * SLOTS, SLOTS), SLOTS)

    mine = rows_of(me)

    def mem_copies(kind, src_of, dst):
        made = []
        for t, (dx, dy) in enumerate(steps):
            peer = peer_of(dx, dy)
            made.append(pltpu.make_async_remote_copy(
                src_ref=src_of(peer), dst_ref=dst,
                send_sem=mem_send.at[kind, t], recv_sem=mem_recv.at[kind, t],
                device_id={"mem": peer}, device_id_type=MESH))
        return made

    xrims = rim_copies(0, xstage, xall)
    erims = rim_copies(1, estage, eall)
    arims = adjoint_copies(astage, aall)
    ccopies = mem_copies(0, lambda peer: colall.at[me], colall.at[me])
    gcopies = mem_copies(1, lambda peer: gsend.at[rows_of(peer), :], grecv.at[mine, :])
    rcopies = mem_copies(2, lambda peer: rall.at[mine, :], rall.at[mine, :])

    far = [(0, 2), (0, n_y - 2)] if len(near) < len(steps) else []
    for dx, dy in far:
        pl.semaphore_signal(far_sem, inc=1, device_id={"mem": peer_of(dx, dy)}, device_id_type=MESH)
    send_strips(xrims)
    start_rims(xrims, (10, 11))
    for c in loads[2]:
        c.wait()
    stage_edges(xstage, ctrl[...], (2, 3))
    start_rims(xrims, (2, 3))

    shift = iota((32, 48), 1) - iota((32, 48), 0)
    for index, (tap, coord) in enumerate(zip((tlon, tlat), column_coords())):
        here = jnp.where(iota((48, EXT), 0) == jnp.broadcast_to(coord, (48, EXT)), 1.0, 0.0).astype(bf16)
        ahead = jnp.zeros((32, 48), f32)
        back = jnp.zeros((32, 48), f32)
        for k in range(TAPS):
            ahead = jnp.where(shift == k, tap[k], ahead)
            back = jnp.where(shift == k, tap[TAPS - 1 - k], back)
        if index == 1:
            back = -descent * back
        back = back.astype(bf16)
        tabs[index] = dot(ahead.astype(bf16), here).astype(bf16)
        tabs[2 + index, :, 0:PAD_C] = dot(back, here[:, OFF_C:EXT]).astype(bf16)
        for d in range(8):
            n = REGIONS[d][3]
            coord = region_coords(d, n)[index]
            rim = jnp.where(iota((48, n), 0) == jnp.broadcast_to(coord, (48, n)), 1.0, 0.0).astype(bf16)
            back_tabs[index, d, :, 0:n] = dot(back, rim).astype(bf16)

    if far:
        pl.semaphore_wait(far_sem, len(far))
    for c in ccopies:
        c.start()
    pass_strips(xrims)
    for c in loads_e:
        c.wait()
    stage_edges(estage, eall[OFF_C:OFF_C + CELLS, :].astype(f32), range(4))
    start_rims(erims, (0, 1, 8, 9, 10, 11))
    start_some(erims, (2, 3), False)
    xall[OFF_C:OFF_C + CELLS, :] = ctrl[...].astype(bf16)

    quality = jnp.zeros((SLOTS, LEV), f32)
    slot = iota((SLOTS, LEV), 0)
    for s in range(SLOTS):
        quality = jnp.where(slot == s, qual[0, 0, 0, s].astype(f32), quality)
    weights = jnp.where(slot < count[0, 0, 0], 0.5 * quality, 0.0)

    for c in ccopies:
        c.wait_recv()
    total = n_mem * SLOTS
    table_i, table_j = by_tile(jnp.concatenate([colall[o] for o in range(n_mem)], axis=0))
    row = iota((total, LEV), 0)
    spread_rows = one_hot(iota((total, 1), 0) >> 4, n_mem)
    lane = iota((total, LEV), 1)
    own_slot = lane == (row & 15)

    def along_rows(table):
        wide = dot(spread_rows, table.astype(f32).astype(bf16))
        return jnp.sum(jnp.where(own_slot, wide, 0.0), axis=1, keepdims=True)

    own_i, own_j = along_rows(table_i), along_rows(table_j)
    lanes = iota((total, 32), 1).astype(f32)
    pick_i = jnp.where(lanes == own_i, 1.0, 0.0).astype(bf16)
    pick_j = jnp.where(lanes == own_j, 1.0, 0.0).astype(bf16)
    for q in range(0, EXT, 128):
        part = dot(pick_i, tabs[0, :, q:q + 128]) * dot(pick_j, tabs[1, :, q:q + 128])
        w2[:, q:q + 128] = part.astype(bf16)

    acc[...] = dot(w2[:, OFF_C:EXT], xall[OFF_C:EXT, :])
    column = jnp.broadcast_to(TILE * own_i + own_j, (total, LEV))
    lane = lane.astype(f32)
    select = jnp.concatenate(
        [jnp.where(lane + float(q) == column, 1.0, 0.0).astype(bf16) for q in range(0, PAD_C, 128)], axis=1)
    ensobs[...] = dot(select, eall[OFF_C:EXT, :])
    for which, row, rows in GROUPS:
        recv_rims(xrims, which)
        acc[...] += dot(w2[:, row:row + rows], xall[row:row + rows, :])
    product = acc[...] * ensobs[...]
    part = product[:, 0:LEV]
    for m in range(1, MEM):
        part = part + product[:, m * LEV:(m + 1) * LEV]
    gsend[...] = part.astype(bf16)
    for c in gcopies:
        c.start()
    start_some(erims, (2, 3), True)
    grecv[mine, :] = gsend[mine, :]

    column_t = jnp.transpose(column)[0:1, :]
    cell = iota((CELLS, total), 0).astype(f32)
    st[...] = jnp.where(cell == jnp.broadcast_to(column_t, (CELLS, total)), 1.0, 0.0).astype(bf16)

    def build(b, _):
        rows = pl.ds(pl.multiple_of(b * 64, 64), 64)
        i, j = by_tile(iota((64, 1), 0) + b * 64)
        at_i, at_j = one_hot(i, 32), one_hot(j, 32)
        for q in range(0, PAD_C, 128):
            part = dot(at_i, tabs[2, :, q:q + 128]) * dot(at_j, tabs[3, :, q:q + 128])
            k2c[rows, q:q + 128] = part.astype(bf16)
        return 0
    lax.fori_loop(0, CELLS // 64, build, 0)
    for d in range(8):
        dz, dl, _, rows = REGIONS[d]
        r = iota((rows, 1), 0)
        i, j = by_tile(r) if dl == 0 else (r >> 3, r & 7)
        i, j = i + (TILE - HALF if dz == 1 else 0), j + (TILE - HALF if dl == 1 else 0)
        part = dot(one_hot(i, 32), back_tabs[0, d, :, 0:rows]) * dot(one_hot(j, 32), back_tabs[1, d, :, 0:rows])
        (k2z, k2l, k2x, k2x)[d // 2][d % 2 if d < 4 else d - 4] = part.astype(bf16)

    for c in gcopies:
        c.wait_recv()
    observed = jnp.zeros((SLOTS, LEV), f32)
    for o in range(n_mem):
        observed = observed + grecv[o * SLOTS:(o + 1) * SLOTS, :].astype(f32)
    residual = weights * (observed - vals[...])
    rall[mine, :] = residual.astype(bf16)
    for c in rcopies:
        c.start()
    pass_strips(erims)
    res_ref[...] = residual
    for m in range(MEM):
        out_ref[m] = (1.0 - descent) * ctrl[:, m * LEV:(m + 1) * LEV].reshape(TILE, TILE, LEV)
    sent_rims(xrims)
    for c in ccopies + gcopies:
        c.wait_send()
    for c in rcopies:
        c.wait_recv()

    adjoint = dot(st[...], rall[...])
    stage_edges(astage, adjoint, range(8))
    start_rims(arims, (4, 5, 6, 7, 2, 3, 0, 1))

    zero = jnp.zeros((PAD_C - CELLS, LEV), f32)
    wide = jnp.concatenate([jnp.concatenate([adjoint, zero], axis=0)] * MEM, axis=1)
    back = dot(k2c[...], (eall[OFF_C:EXT, :].astype(f32) * wide).astype(bf16))
    for m in range(MEM):
        out_ref[m] += back[:, m * LEV:(m + 1) * LEV].reshape(TILE, TILE, LEV)
    recv_rims(erims, (2, 3, 4, 5, 6, 7, 10, 11))
    sent_rims(erims)
    for c in rcopies:
        c.wait_send()
    for d in (2, 3, 0, 1, 4, 5, 6, 7):
        recv_rims(arims, (d,))
        row, rows = REGIONS[d][2:]
        matrix = (k2z, k2l, k2x, k2x)[d // 2][d % 2 if d < 4 else d - 4]
        back = dot(matrix, eall[row:row + rows, :] * jnp.concatenate([aall[row:row + rows, :]] * MEM, axis=1))
        for m in range(MEM):
            block = block_of(out_ref, m, d)
            block[...] += back[:, m * LEV:(m + 1) * LEV].reshape(block.shape)

    sent_rims(arims)


def write(a_ref, b_ref, a_out, b_out, sem):
    copies = [pltpu.make_async_copy(a_ref, a_out, sem.at[0]), pltpu.make_async_copy(b_ref, b_out, sem.at[1])]
    for c in copies:
        c.start()
    for c in copies:
        c.wait()


def shards(sizes, controls, ensemble, taps_lon, taps_lat, obs_columns, obs_count, obs_quality, obs_values):
    n_mem = sizes[2]
    total = n_mem * SLOTS
    vmem = pl.BlockSpec(memory_space=pltpu.VMEM)
    hbm = pl.BlockSpec(memory_space=pltpu.HBM)
    shapes = (jax.ShapeDtypeStruct((MEM, TILE, TILE, LEV), f32), jax.ShapeDtypeStruct((SLOTS, LEV), f32))
    results = pl.pallas_call(
        functools.partial(kernel, sizes),
        out_shape=shapes,
        in_specs=[hbm] * 5 + [pl.BlockSpec(memory_space=pltpu.SMEM)] + [hbm] * 2,
        out_specs=(vmem, vmem),
        scratch_shapes=[
            pltpu.VMEM((CELLS, WIDE), f32),
            pltpu.VMEM((EXT, WIDE), bf16),
            pltpu.VMEM((EXT, WIDE), bf16),
            pltpu.VMEM((EXT, LEV), bf16),
            pltpu.VMEM((OFF_X, WIDE), bf16),
            pltpu.VMEM((OFF_X, WIDE), bf16),
            pltpu.VMEM((OFF_C, LEV), bf16),
            pltpu.VMEM((n_mem, 1, LEV), jnp.int32),
            pltpu.VMEM((total, LEV), bf16),
            pltpu.VMEM((total, LEV), bf16),
            pltpu.VMEM((total, LEV), bf16),
            pltpu.VMEM((total, EXT), bf16),
            pltpu.VMEM((CELLS, PAD_C), bf16),
            pltpu.VMEM((2, SIDE, SIDE), bf16),
            pltpu.VMEM((2, SIDE, SIDE), bf16),
            pltpu.VMEM((4, CORNER, CORNER), bf16),
            pltpu.VMEM((CELLS, total), bf16),
            pltpu.VMEM((4, 32, EXT), bf16),
            pltpu.VMEM((2, 8, 32, SIDE), bf16),
            pltpu.VMEM((total, WIDE), f32),
            pltpu.VMEM((total, WIDE), f32),
            pltpu.SMEM((TAPS,), f32),
            pltpu.SMEM((TAPS,), f32),
            pltpu.SMEM((1, 1, 1, SLOTS), jnp.int32),
            pltpu.SMEM((1, 1, 1, SLOTS), jnp.int32),
            pltpu.VMEM((SLOTS, LEV), f32),
            pltpu.SemaphoreType.DMA((4, MEM)),
            pltpu.SemaphoreType.DMA((5,)),
            pltpu.SemaphoreType.DMA((3, 12)),
            pltpu.SemaphoreType.DMA((3, 12)),
            pltpu.SemaphoreType.DMA((3, n_mem)),
            pltpu.SemaphoreType.DMA((3, n_mem)),
            pltpu.SemaphoreType.REGULAR,
        ],
        compiler_params=pltpu.CompilerParams(collective_id=0, has_side_effects=True, vmem_limit_bytes=30 * 1024 * 1024),
        name="step",
    )(*[x if x.size == 1 else pltpu.with_memory_space_constraint(x, pltpu.HBM) for x in (
        controls.reshape(MEM, CELLS, LEV),
        ensemble.reshape(MEM, CELLS, LEV),
        taps_lon,
        taps_lat,
        obs_columns,
        obs_count,
        obs_quality,
        obs_values.reshape(SLOTS, LEV),
    )])
    new_controls, residual = pl.pallas_call(
        write,
        out_shape=shapes,
        in_specs=[pl.BlockSpec(memory_space=pl.ANY)] * 2,
        out_specs=(hbm, hbm),
        scratch_shapes=[pltpu.SemaphoreType.DMA((2,))],
        compiler_params=pltpu.CompilerParams(vmem_limit_bytes=1 << 20),
        name="write",
    )(*results)
    return new_controls, residual.reshape(obs_values.shape)


def solution(mesh):
    sizes = (mesh.shape["lon"], mesh.shape["lat"], mesh.shape["mem"])
    placed = (
        P("mem", "lon", "lat", None),
        P("mem", "lon", "lat", None),
        P(),
        P(),
        P("lon", "lat", "mem", None),
        P("lon", "lat", "mem"),
        P("lon", "lat", "mem", None),
        P("lon", "lat", "mem", None, None),
    )
    return jax.shard_map(
        functools.partial(shards, sizes),
        mesh=mesh,
        in_specs=placed,
        out_specs=(P("mem", "lon", "lat", None), P("lon", "lat", "mem", None, None)),
        check_vma=False,
    )
```
